256 devices in a mesh: expert: 16 (over x, y), edata: 16 (over z, core).
Axes of the slice: x: 4, y: 4, z: 8, core: 2. Of those that a mesh axis runs over, the one named last changes fastest.
Arguments:
- tokens: bfloat16 [1024, 7168], P(('expert', 'edata')), may hold values from -8 to 8
- routes: int32 [1024, 8], P(('expert', 'edata')), may hold values from 0 to 31, all different within a row; in each aligned block of 4 rows (0 to 3, 4 to 7, ...) at most 2 rows name the same one
- combine: bfloat16 [1024, 8], P(('expert', 'edata')), may hold values from 0.049804688 to 0.5
- w_gate: bfloat16 [32, 7168, 2048], P('expert', None, 'edata'), may hold values from -0.0625 to 0.0625
- w_up: bfloat16 [32, 7168, 2048], P('expert', None, 'edata')
- w_down: bfloat16 [32, 2048, 7168], P('expert', 'edata'), may hold values from -0.125 to 0.125
- past_amax: float32 [32], P('expert'), may hold values from 10 to 300
Outputs:
- layer_out: bfloat16 [1024, 7168], P(('expert', 'edata'))
- hidden_amax: float32 [32], P('expert')
The draws below stay inside these ranges and needn't reach their ends.
Inputs may be any that keep to these rules, and one draw needn't show every extreme that they name: `routes`: each row names 8 different experts and every expert is named by some token. Among the 4 tokens of one device no expert is named more than 2 times, a bound that some block reaches.
All inputs are finite; a program needn't handle non-finite values.
Results may differ from the reference program's by a relative error of at most 0.018.
Values may be sent and summed in bfloat16 or wider, within the bound.
No kernel may reach another device: no remote copies, remote signals or barrier semaphores. Data moves between devices by JAX's collectives and lax.ppermute only.
A program may use at most 128 MiB of HBM per device.

```python
import math
import jax
import jax.numpy as jnp
import numpy as np
from jax import lax

D = 7168
F = 2048
TOP = 8
TOK_DEV = 4
EXPERTS = 32
F_DEV = 128
CAP = 2
TOKENS = 1024
N_EDATA = 16


def draw_tokens(key, part):
    own_key = jax.random.fold_in(key, 11)
    key_scale, key_noise = jax.random.split(own_key, 2)
    row_scale = jnp.exp(jax.random.uniform(key_scale, (TOKENS, 1), jnp.float32, math.log(0.5), math.log(1.6)))
    values = row_scale * jax.random.normal(key_noise, (TOKENS, D), jnp.float32)
    return jnp.clip(values, -8.0, 8.0).astype(jnp.bfloat16)


def draw_w_up(key, part):
    own_key = jax.random.fold_in(key, 23)
    key_column, key_noise = jax.random.split(own_key)
    column_scale = jnp.exp(jax.random.uniform(key_column, (EXPERTS, 1, F), jnp.float32, math.log(0.4), math.log(4.0)))
    noise_part = jnp.clip(jax.random.normal(key_noise, (EXPERTS, D, F), jnp.float32), -6.0, 6.0)
    return (column_scale * noise_part / math.sqrt(D)).astype(jnp.bfloat16)


def steps_of(key, extent, pieces, low, top_value):
    def one(dim, shards_of):
        draws = jax.random.uniform(jax.random.fold_in(jax.random.fold_in(key, 6), dim), (shards_of,), jnp.float32, low / len(pieces), top_value / len(pieces))
        return jnp.repeat(jnp.exp(draws), extent[dim] // shards_of).reshape((-1,) + (1,) * (len(extent) - dim - 1))

    factor_of = one(*pieces[0])
    for cut in pieces[1:]:
        factor_of = factor_of * one(*cut)
    return factor_of


def assign_block(key, own, number, rows, number_of, top, most, skew):
    order = jax.random.permutation(key, number_of)
    packed, usual = load_shares(number_of, rows * top, most, skew, True), load_shares(number_of, rows * top, most, skew, False)
    places = jnp.arange(number_of)

    def named(sizes, rotation):
        used = int((sizes > 0).sum())
        fixed = max(1, used // 4)
        shifted = fixed + (places - fixed + rotation * (used - fixed)) % max(1, number_of - fixed)
        return jnp.zeros((number_of,), jnp.int32).at[order[jnp.where(places < fixed, places, shifted)]].set(jnp.asarray(sizes, jnp.int32))

    sizes = jnp.where(number % 4 == 0, named(packed, number // 4), named(usual, number - number // 4 - 1))
    mixed = jax.random.permutation(jax.random.fold_in(own, 3), number_of)
    source_of, receiver = mixed[0:number_of // 2 * 2:2], mixed[1:number_of // 2 * 2:2]
    slack = jnp.minimum(sizes[source_of] - 1, most - sizes[receiver]) // 2
    slack = jnp.where((source_of == order[0]) | (receiver == order[0]) | (sizes[receiver] == 0), 0, jnp.maximum(slack, 0))
    shifted = jax.random.randint(jax.random.fold_in(own, 4), (number_of // 2,), 0, 1 << 20) % (slack + 1)
    sizes = sizes.at[source_of].add(-shifted).at[receiver].add(shifted)
    labels = jnp.searchsorted(jnp.cumsum(sizes), jnp.arange(rows * top), side="right").astype(jnp.int32)
    table = labels.reshape(top, rows).T
    table = table[jax.random.permutation(jax.random.fold_in(own, 1), rows)]
    rotation = jax.random.randint(jax.random.fold_in(own, 2), (rows, 1), 0, top)
    return jnp.take_along_axis(table, (jnp.arange(top)[None, :] + rotation) % top, axis=1)


def load_shares(count, total, limit, skew, full):
    loads = [(1 << 20) // math.isqrt(grade ** skew) + 1 for grade in range(1, count + 1)]
    largest = limit if full else min(limit, max(-(-total // count), total * loads[0] // sum(loads)))
    least = 1 if total - largest >= count - 1 else 0
    given, spare = [largest] + [least] * (count - 1), total - largest - least * (count - 1)
    while spare > 0:
        free = [i for i in range(1, count) if given[i] < largest] or [i for i in range(1, count) if given[i] < limit]
        pool, left = sum([loads[i] for i in free]), spare
        for i in free:
            extra = min(limit - given[i], max(1, left * loads[i] // pool), spare)
            given[i] = given[i] + extra
            spare = spare - extra
    return np.array(given)


def bell_draw(stream_key, dims, width, most, shards=(), kind=jnp.bfloat16):
    array = jax.random.normal(stream_key, dims, jnp.float32) * width
    if len(shards) > 0:
        array = steps_of(stream_key, dims, shards, -0.22, 0.18) * array
    return jnp.clip(array, min=-most, max=most).astype(kind)


def setup_inputs(seed: int = 0) -> dict:
    arg_keys = jax.random.split(jax.random.key(seed), 8)
    tokens = draw_tokens(jax.random.fold_in(arg_keys[7], 71), 0)
    routes_keys = jax.random.split(jax.random.fold_in(arg_keys[1], 1), TOKENS // TOK_DEV)
    routes_turns = jax.random.permutation(jax.random.fold_in(arg_keys[1], 3), TOKENS // TOK_DEV)
    routes = jax.vmap(lambda own, number: assign_block(jax.random.fold_in(arg_keys[1], 2), own, number, TOK_DEV, EXPERTS, TOP, CAP, 2))(routes_keys, routes_turns).reshape((TOKENS, TOP))
    combine = jnp.clip(0.049804688 + 0.4501953 * jax.random.uniform(arg_keys[2], (TOKENS, TOP), jnp.float32) ** steps_of(arg_keys[2], (TOKENS, TOP), ((0, 256),), -0.2, 0.2), 0.049804688, 0.5).astype(jnp.bfloat16)
    w_gate = bell_draw(arg_keys[3], (EXPERTS, D, F), D ** -0.5, 0.0625, ((0, 16), (2, 16)))
    w_up = draw_w_up(jax.random.fold_in(arg_keys[7], 71), 0)
    w_down = bell_draw(arg_keys[5], (EXPERTS, F, D), F ** -0.5, 0.125, ((0, 16), (1, 16)))
    past_amax = jnp.clip(jnp.exp(math.log(300.0) - 3.4011974 * jax.random.uniform(arg_keys[6], (EXPERTS,), jnp.float32) ** steps_of(arg_keys[6], (EXPERTS,), ((0, 16),), -0.2, 0.2)), 10.0, 300.0)
    return dict(tokens=tokens, routes=routes, combine=combine, w_gate=w_gate, w_up=w_up, w_down=w_down, past_amax=past_amax)


quant_limit = 448.0
tile_rows = 128


def reference(tokens, routes, combine, w_gate, w_up, w_down, past_amax):
    pair_count = TOKENS * TOP
    flat_routes = routes.reshape(pair_count)
    expert_hits = (flat_routes[:, None] == jnp.arange(EXPERTS, dtype=jnp.int32)[None, :]).astype(jnp.int32)
    counts = jnp.sum(expert_hits, axis=0)
    padded = (counts + tile_rows - 1) // tile_rows * tile_rows
    block_ends = jnp.cumsum(padded)
    starts = block_ends - padded
    before = jnp.cumsum(expert_hits, axis=0) - expert_hits
    slot_rank = jnp.sum(expert_hits * before, axis=1)
    slot_dest = jnp.sum(expert_hits * starts[None, :], axis=1) + slot_rank
    block_count = (pair_count + tile_rows - 1) // tile_rows + EXPERTS
    slot_pair = jnp.full((block_count * tile_rows,), -1, jnp.int32).at[slot_dest].set(
        jnp.arange(pair_count, dtype=jnp.int32))
    block_start = jnp.arange(block_count, dtype=jnp.int32) * tile_rows
    block_expert = jnp.minimum(
        jnp.sum((block_ends[None, :] <= block_start[:, None]).astype(jnp.int32), axis=1), EXPERTS - 1)
    flat_weight = combine.reshape(pair_count).astype(jnp.float32)
    quant_gain = quant_limit / past_amax
    dequant = past_amax / quant_limit

    def block_step(loop_state, block_index):
        accumulated, amax_table = loop_state
        pair_rows = lax.dynamic_slice_in_dim(slot_pair, block_index * tile_rows, tile_rows)
        occupied = pair_rows >= 0
        pair_safe = jnp.maximum(pair_rows, 0)
        token_index = pair_safe // TOP
        expert_id = block_expert[block_index]
        inputs = tokens[token_index]
        gate_proj = jnp.dot(inputs, w_gate[expert_id], preferred_element_type=jnp.float32)
        up_proj = jnp.dot(inputs, w_up[expert_id], preferred_element_type=jnp.float32)
        hidden = jax.nn.silu(gate_proj) * up_proj
        hidden = jnp.where(occupied[:, None], hidden, 0.0)
        amax_table = amax_table.at[expert_id].max(jnp.max(jnp.abs(hidden)))
        quantized = jnp.clip(hidden * quant_gain[expert_id], -quant_limit, quant_limit).astype(jnp.bfloat16)
        grouped = quantized.reshape(tile_rows, N_EDATA, F_DEV).astype(jnp.float32)
        down_table = w_down[expert_id].reshape(N_EDATA, F_DEV, D).astype(jnp.float32)
        part_rows = jnp.einsum("rgf,gfd->rgd", grouped, down_table,
                               precision=lax.Precision.HIGHEST) * dequant[expert_id]
        part_rows = lax.optimization_barrier(part_rows.astype(jnp.bfloat16)).astype(jnp.float32)
        expert_out = jnp.sum(part_rows, axis=1)
        pair_weight = jnp.where(occupied, flat_weight[pair_safe], 0.0)
        accumulated = accumulated.at[token_index].add(pair_weight[:, None] * expert_out)
        return (accumulated, amax_table), None

    start_state = (jnp.zeros((TOKENS, D), jnp.float32), jnp.zeros((EXPERTS,), jnp.float32))
    final_state, unused = lax.scan(block_step, start_state, jnp.arange(block_count, dtype=jnp.int32))
    accumulated, amax_table = final_state
    return (accumulated.astype(jnp.bfloat16), amax_table)
```

```python
import jax
import jax.numpy as jnp
from jax import lax
from jax.sharding import PartitionSpec as P

quant_limit = 448.0
lane = 128


def per_device(tokens, routes, combine, w_gate, w_up, w_down, past_amax):
    groups = lax.axis_size("expert")
    members = lax.axis_size("edata")
    local_experts, model_width, hidden_units = w_gate.shape
    rows = tokens.shape[0]
    half = model_width // 2
    fan = local_experts * hidden_units
    experts = groups * local_experts
    core = lax.axis_index("edata") % 2
    group = lax.axis_index("expert")
    swap = [(i, i ^ 1) for i in range(members)]

    lanes = jnp.arange(lane, dtype=jnp.int32)
    hits = routes[:, :, None] == lanes[None, None, :]
    weights = jnp.sum(jnp.where(hits, combine.astype(jnp.float32)[:, :, None], 0.0), axis=1)
    weights = weights.astype(jnp.bfloat16)

    pieces = jnp.stack(
        [
            jnp.concatenate([tokens[:, :half], weights], axis=1),
            jnp.concatenate([tokens[:, half:], weights], axis=1),
        ]
    )
    outgoing = jnp.broadcast_to(
        pieces[None], (members // 2, 2, rows, half + lane)
    ).reshape(members, rows, half + lane)
    line = lax.all_to_all(outgoing, "edata", split_axis=0, concat_axis=0, tiled=True)
    line = line.reshape(members * rows, half + lane)
    line, w_gate, w_up, w_down = lax.optimization_barrier((line, w_gate, w_up, w_down))
    everyone = lax.all_gather(line, "expert", axis=0, tiled=True)

    def mine_and_other(w, axis):
        keep = lax.dynamic_slice_in_dim(w, core * half, half, axis=axis)
        give = lax.dynamic_slice_in_dim(w, (1 - core) * half, half, axis=axis)
        return keep, lax.ppermute(give, "edata", swap)

    gate_keep, gate_got = mine_and_other(w_gate, 1)
    up_keep, up_got = mine_and_other(w_up, 1)
    down_keep, down_got = mine_and_other(w_down, 2)

    def side(w):
        return [w[j] for j in range(local_experts)]

    w_other = jnp.concatenate(side(gate_got) + side(up_got), axis=1)
    w_own_gate = jnp.concatenate(side(gate_keep), axis=1)
    w_own_up = jnp.concatenate(side(up_keep), axis=1)
    w_out = jnp.concatenate(
        [down_keep.reshape(fan, half), down_got.reshape(fan, half)], axis=0
    )

    everyone, w_other, w_own_gate, w_own_up, w_out = lax.optimization_barrier(
        (everyone, w_other, w_own_gate, w_own_up, w_out)
    )
    features = everyone[:, :half]

    unit_expert = jnp.arange(fan, dtype=jnp.int32) // hidden_units
    spread = (lanes[:, None] == group * local_experts + unit_expert[None, :]).astype(jnp.bfloat16)
    quant_gain = jnp.repeat(quant_limit / past_amax, hidden_units)
    dequant = jnp.repeat(past_amax / quant_limit, hidden_units)

    other = jnp.dot(features, w_other, preferred_element_type=jnp.float32)
    got = lax.ppermute(other, "edata", swap)
    weight = jnp.dot(everyone[:, half:], spread, preferred_element_type=jnp.float32)
    own_gate = jnp.dot(features, w_own_gate, preferred_element_type=jnp.float32)
    own_up = jnp.dot(features, w_own_up, preferred_element_type=jnp.float32)
    gate_proj = own_gate + got[:, :fan]
    up_proj = own_up + got[:, fan:]
    hidden = jax.nn.silu(gate_proj) * up_proj
    peaks = jnp.max(jnp.where(weight > 0.0, jnp.abs(hidden), 0.0), axis=0)
    peaks = jnp.max(peaks.reshape(local_experts, hidden_units), axis=1)
    clipped = jnp.clip(hidden * quant_gain[None, :], -quant_limit, quant_limit)
    scaled = (clipped * (weight * dequant[None, :])).astype(jnp.bfloat16)
    both = jnp.concatenate([scaled, lax.ppermute(scaled, "edata", swap)], axis=1)
    down = jnp.dot(both, w_out, preferred_element_type=jnp.float32).astype(jnp.bfloat16)
    reduced = lax.psum_scatter(down, "expert", scatter_dimension=0, tiled=True)
    hidden_amax = lax.pmax(peaks, "edata")
    reduced, hidden_amax = lax.optimization_barrier((reduced, hidden_amax))
    reduced = reduced.reshape(members, rows, half)
    back = lax.all_to_all(reduced, "edata", split_axis=0, concat_axis=0, tiled=True)
    total = jnp.sum(back.reshape(members // 2, 2, rows, half).astype(jnp.float32), axis=0)
    layer_out = jnp.concatenate([total[0], total[1]], axis=1)
    return (layer_out.astype(jnp.bfloat16), hidden_amax)


def solution(mesh):
    return jax.shard_map(
        per_device,
        mesh=mesh,
        in_specs=(
            P(("expert", "edata"), None),
            P(("expert", "edata"), None),
            P(("expert", "edata"), None),
            P("expert", None, "edata"),
            P("expert", None, "edata"),
            P("expert", "edata", None),
            P("expert"),
        ),
        out_specs=(P(("expert", "edata"), None), P("expert")),
        check_vma=False,
    )
```

```python
import jax
import jax.numpy as jnp
from jax import lax
from jax.sharding import PartitionSpec as P

quant_limit = 448.0
lane = 128
ring = 4


def per_device(tokens, routes, combine, w_gate, w_up, w_down, past_amax):
    groups = lax.axis_size("expert")
    members = lax.axis_size("edata")
    local_experts, model_width, hidden_units = w_gate.shape
    rows = tokens.shape[0]
    half = model_width // 2
    side_width = half // 2
    fan = local_experts * hidden_units
    depth = members // 2
    core = lax.axis_index("edata") % 2
    group = lax.axis_index("expert")
    swap = [(i, i ^ 1) for i in range(members)]

    def pair(v):
        return lax.ppermute(v, "edata", swap)

    def to_z(v, k):
        return lax.ppermute(v, "edata", [(i, (i + 2 * k) % members) for i in range(members)])

    def to_x(v, k):
        return lax.ppermute(
            v, "expert", [(e, (e // ring + k) % ring * ring + e % ring) for e in range(groups)]
        )

    def to_y(v, k):
        return lax.ppermute(
            v, "expert", [(e, e // ring * ring + (e % ring + k) % ring) for e in range(groups)]
        )

    def ring_gather(send, block):
        cut = block.shape[0] // 2
        behind = send(block, 1)
        ahead = send(block, -1)
        far = [send(behind[:cut], 1), send(ahead[cut:], -1)]
        return [block, ahead, jnp.concatenate(far, axis=0), behind]

    def add(*parts):
        return sum(p.astype(jnp.float32) for p in parts).astype(jnp.bfloat16)

    def ring_scatter(send, blocks):
        cut = blocks[0].shape[0] // 2
        low, high = [b[:cut] for b in blocks], [b[cut:] for b in blocks]
        far_low = send(low[2], 1)
        far_high = send(high[2], -1)
        got_high = [send(high[1], 1)]
        got_low = [send(low[3], -1)]
        got_low.append(send(add(low[1], far_low), 1))
        got_high.append(send(add(high[3], far_high), -1))
        return jnp.concatenate([add(low[0], *got_low), add(high[0], *got_high)], axis=0)

    lanes = jnp.arange(lane, dtype=jnp.int32)
    hits = routes[:, :, None] == lanes[None, None, :]
    weights = jnp.sum(jnp.where(hits, combine.astype(jnp.float32)[:, :, None], 0.0), axis=1)
    weights = weights.astype(jnp.bfloat16)

    first = core == 0

    def by_core(own, got, axis):
        return jnp.where(
            first, jnp.concatenate([own, got], axis=axis), jnp.concatenate([got, own], axis=axis)
        )

    left, right = tokens[:, :half], tokens[:, half:]
    keep = jnp.concatenate([jnp.where(first, left, right), weights], axis=1)
    give = jnp.concatenate([jnp.where(first, right, left), weights], axis=1)
    chip = by_core(keep, pair(give), 0)

    line = [chip] + [None] * (depth - 1)
    for k in range(1, depth):
        line[depth - k] = to_z(chip, k)
    line = jnp.concatenate(line, axis=0)
    line_rows = line.shape[0]
    plane_a = jnp.concatenate(ring_gather(to_y, line[:, :side_width]), axis=0)
    plane_b = jnp.concatenate(ring_gather(to_x, line[:, side_width:]), axis=0)
    plane_a, plane_b, w_gate, w_up, w_down = lax.optimization_barrier(
        (plane_a, plane_b, w_gate, w_up, w_down)
    )
    all_a = jnp.concatenate(ring_gather(to_x, plane_a), axis=0)
    all_b = jnp.concatenate(
        [b.reshape(ring, 1, line_rows, -1) for b in ring_gather(to_y, plane_b)], axis=1
    )
    everyone = jnp.concatenate([all_a, all_b.reshape(all_a.shape[0], -1)], axis=1)

    def mine_and_other(w, axis):
        keep = lax.dynamic_slice_in_dim(w, core * half, half, axis=axis)
        give = lax.dynamic_slice_in_dim(w, (1 - core) * half, half, axis=axis)
        return keep, pair(give)

    gate_keep, gate_got = mine_and_other(w_gate, 1)
    up_keep, up_got = mine_and_other(w_up, 1)
    down_keep, down_got = mine_and_other(w_down, 2)

    def side(w):
        return [w[j] for j in range(local_experts)]

    w_other = jnp.concatenate(side(gate_got) + side(up_got), axis=1)
    w_own_gate = jnp.concatenate(side(gate_keep), axis=1)
    w_own_up = jnp.concatenate(side(up_keep), axis=1)
    w_out = jnp.concatenate(
        [down_keep.reshape(fan, half), down_got.reshape(fan, half)], axis=0
    )
    everyone, w_other, w_own_gate, w_own_up, w_out = lax.optimization_barrier(
        (everyone, w_other, w_own_gate, w_own_up, w_out)
    )
    features = everyone[:, :half]

    unit_expert = jnp.arange(fan, dtype=jnp.int32) // hidden_units
    spread = (lanes[:, None] == group * local_experts + unit_expert[None, :]).astype(jnp.bfloat16)
    quant_gain = jnp.repeat(quant_limit / past_amax, hidden_units)
    dequant = jnp.repeat(past_amax / quant_limit, hidden_units)

    other = jnp.dot(features, w_other, preferred_element_type=jnp.float32)
    got = pair(other)
    weight = jnp.dot(everyone[:, half:], spread, preferred_element_type=jnp.float32)
    own_gate = jnp.dot(features, w_own_gate, preferred_element_type=jnp.float32)
    own_up = jnp.dot(features, w_own_up, preferred_element_type=jnp.float32)
    gate_proj = own_gate + got[:, :fan]
    up_proj = own_up + got[:, fan:]
    hidden = jax.nn.silu(gate_proj) * up_proj
    peaks = jnp.max(jnp.where(weight > 0.0, jnp.abs(hidden), 0.0), axis=0)
    peaks = jnp.pad(peaks.reshape(local_experts, hidden_units), ((0, 0), (0, lane - hidden_units)))
    clipped = jnp.clip(hidden * quant_gain[None, :], -quant_limit, quant_limit)
    scaled = (clipped * (weight * dequant[None, :])).astype(jnp.bfloat16)
    both = jnp.concatenate([scaled, pair(scaled)], axis=1)
    down = jnp.dot(both, w_out, preferred_element_type=jnp.float32).astype(jnp.bfloat16)

    down = down.reshape(ring, ring, line_rows, half)
    plane_a = ring_scatter(
        to_x, [down[k, :, :, :side_width].reshape(-1, side_width) for k in range(ring)]
    )
    plane_b = ring_scatter(
        to_y, [down[:, k, :, side_width:].reshape(-1, side_width) for k in range(ring)]
    )
    line_a = ring_scatter(
        to_y, [plane_a[k * line_rows : (k + 1) * line_rows] for k in range(ring)]
    )
    line_b = ring_scatter(
        to_x, [plane_b[k * line_rows : (k + 1) * line_rows] for k in range(ring)]
    )

    def split(v):
        top = lax.reduce_precision(v, 8, 7)
        return jnp.concatenate([top, v - top], axis=0).astype(jnp.bfloat16)

    def joined(v):
        v = v.astype(jnp.float32)
        return v[:local_experts] + v[local_experts : 2 * local_experts]

    chip_rows = 2 * rows
    tail = jnp.pad(split(peaks), ((0, chip_rows - 2 * local_experts), (0, 0)))
    tail = jnp.broadcast_to(tail[None], (depth, chip_rows, lane)).reshape(line_rows, lane)
    message = jnp.concatenate([line_a, line_b, tail], axis=1)
    arrived = [message[:chip_rows]]
    for k in range(1, depth):
        arrived.append(to_z(message[k * chip_rows : (k + 1) * chip_rows], k))
    total = sum(a[:, :half].astype(jnp.float32) for a in arrived).astype(jnp.bfloat16)
    for a in arrived[1:]:
        peaks = jnp.maximum(peaks, joined(a[:, half:]))
    mine = jnp.where(first, total[:rows], total[rows:])
    give = jnp.where(first, total[rows:], total[:rows])
    theirs = pair(jnp.concatenate([give, split(peaks)], axis=1))
    layer_out = by_core(mine, theirs[:, :half], 1)
    hidden_amax = jnp.max(jnp.maximum(peaks, joined(theirs[:, half:])), axis=1)
    return (layer_out, hidden_amax)


def solution(mesh):
    return jax.shard_map(
        per_device,
        mesh=mesh,
        in_specs=(
            P(("expert", "edata"), None),
            P(("expert", "edata"), None),
            P(("expert", "edata"), None),
            P("expert", None, "edata"),
            P("expert", None, "edata"),
            P("expert", "edata", None),
            P("expert"),
        ),
        out_specs=(P(("expert", "edata"), None), P("expert")),
        check_vma=False,
    )
```

```python
import jax
import jax.numpy as jnp
from jax import lax
from jax.sharding import PartitionSpec as P


quant_limit = 448.0
lane = 128
ring = 4


def per_device(tokens, routes, combine, w_gate, w_up, w_down, past_amax):
    groups = lax.axis_size("expert")
    members = lax.axis_size("edata")
    local_experts, model_width, hidden_units = w_gate.shape
    rows = tokens.shape[0]
    half = model_width // 2
    side_width = half // 2
    fan = local_experts * hidden_units
    core = lax.axis_index("edata") % 2
    group = lax.axis_index("expert")
    swap = [(i, i ^ 1) for i in range(members)]

    def pair(v):
        return lax.ppermute(v, "edata", swap)

    def to_x(v, k):
        return lax.ppermute(
            v, "expert", [(e, (e // ring + k) % ring * ring + e % ring) for e in range(groups)]
        )

    def to_y(v, k):
        return lax.ppermute(
            v, "expert", [(e, e // ring * ring + (e % ring + k) % ring) for e in range(groups)]
        )

    def small_gather(send, block):
        behind = send(block, 1)
        return [block, send(block, -1), send(behind, 1), behind]

    def ring_gather(sends, blocks, ready):
        near = [(send(block, 1), send(block, -1)) for send, block in zip(sends, blocks)]
        near, ready = lax.optimization_barrier((near, ready))
        gathered = []
        for send, block, (behind, ahead) in zip(sends, blocks, near):
            cut = block.shape[0] // 2
            far = [send(behind[:cut], 1), send(ahead[cut:], -1)]
            gathered.append([block, ahead, jnp.concatenate(far, axis=0), behind])
        return gathered, ready

    def add(*parts):
        return sum(p.astype(jnp.float32) for p in parts).astype(jnp.bfloat16)

    def small_scatter(send, blocks):
        behind = send(blocks[3], -1)
        return add(blocks[0], behind, send(add(blocks[1], send(blocks[2], 1)), 1))

    def ring_scatter(send, blocks):
        cut = blocks[0].shape[0] // 2
        far_low = send(blocks[2][:cut], 1)
        far_high = send(blocks[2][cut:], -1)
        ahead = jnp.concatenate([add(blocks[1][:cut], far_low), blocks[1][cut:]], axis=0)
        behind = jnp.concatenate([blocks[3][:cut], add(blocks[3][cut:], far_high)], axis=0)
        return add(blocks[0], send(ahead, 1), send(behind, -1))

    lanes = jnp.arange(lane, dtype=jnp.int32)
    hits = routes[:, :, None] == lanes[None, None, :]
    weights = jnp.sum(jnp.where(hits, combine.astype(jnp.float32)[:, :, None], 0.0), axis=1)
    weights = weights.astype(jnp.bfloat16)

    pieces = jnp.stack(
        [
            jnp.concatenate([tokens[:, :half], weights], axis=1),
            jnp.concatenate([tokens[:, half:], weights], axis=1),
        ]
    )
    outgoing = jnp.broadcast_to(pieces[None], (members // 2, 2, rows, half + lane))
    outgoing = outgoing.reshape(members, rows, half + lane)
    line = lax.all_to_all(outgoing, "edata", split_axis=0, concat_axis=0, tiled=True)
    line = line.reshape(members * rows, half + lane)
    line_rows = members * rows

    plane_a = jnp.concatenate(small_gather(to_y, line[:, :side_width]), axis=0)
    plane_b = jnp.concatenate(small_gather(to_x, line[:, side_width:]), axis=0)
    plane_a, plane_b, w_gate, w_up, w_down = lax.optimization_barrier(
        (plane_a, plane_b, w_gate, w_up, w_down)
    )

    def joined_half(side):
        cut = [
            lax.dynamic_slice_in_dim(w, side * half, half, axis=1)[j]
            for w in (w_gate, w_up)
            for j in range(local_experts)
        ]
        return jnp.concatenate(cut, axis=1)

    def down_half(side):
        return lax.dynamic_slice_in_dim(w_down, side * half, half, axis=2).reshape(fan, half)

    w_own = joined_half(core)
    other_half = joined_half(1 - core)
    other_down = down_half(1 - core)
    w_other = pair(other_half)
    down_got = pair(other_down)
    down_own = down_half(core)

    (blocks_a, blocks_b), (w_own, down_own, down_got) = ring_gather(
        (to_x, to_y), (plane_a, plane_b), (w_own, down_own, down_got)
    )
    w_out = jnp.concatenate([down_own, down_got], axis=0)
    all_a = jnp.concatenate(blocks_a, axis=0)
    all_b = jnp.zeros((ring, ring, line_rows, half + lane - side_width), jnp.bfloat16)
    for k, block in enumerate(blocks_b):
        all_b = lax.dynamic_update_slice(
            all_b, block.reshape(ring, 1, line_rows, -1), (0, k, 0, 0)
        )
    all_b = all_b.reshape(all_a.shape[0], -1)
    rest = half - side_width

    def project(w):
        return jnp.dot(
            all_a, w[:side_width], preferred_element_type=jnp.float32
        ) + jnp.dot(all_b[:, :rest], w[side_width:], preferred_element_type=jnp.float32)

    unit_expert = jnp.arange(fan, dtype=jnp.int32) // hidden_units
    spread = (lanes[:, None] == group * local_experts + unit_expert[None, :]).astype(jnp.bfloat16)
    quant_gain = jnp.repeat(quant_limit / past_amax, hidden_units)
    dequant = jnp.repeat(past_amax / quant_limit, hidden_units)

    got = pair(project(w_other))
    weight = jnp.dot(all_b[:, rest:], spread, preferred_element_type=jnp.float32)
    both_proj = project(w_own) + got
    gate_proj = both_proj[:, :fan]
    up_proj = both_proj[:, fan:]
    hidden = jax.nn.silu(gate_proj) * up_proj
    peaks = jnp.max(jnp.where(weight > 0.0, jnp.abs(hidden), 0.0), axis=0)
    peaks = jnp.pad(peaks.reshape(local_experts, hidden_units), ((0, 0), (0, lane - hidden_units)))
    clipped = jnp.clip(hidden * quant_gain[None, :], -quant_limit, quant_limit)
    scaled = (clipped * (weight * dequant[None, :])).astype(jnp.bfloat16)
    both = jnp.concatenate([scaled, pair(scaled)], axis=1)
    down = jnp.dot(both, w_out, preferred_element_type=jnp.float32).astype(jnp.bfloat16)

    down = down.reshape(ring, ring, line_rows, half)
    plane_a = ring_scatter(
        to_x, [down[k, :, :, :side_width].reshape(-1, side_width) for k in range(ring)]
    )
    plane_b = ring_scatter(
        to_y, [down[:, k, :, side_width:].reshape(-1, side_width) for k in range(ring)]
    )
    line_a = small_scatter(
        to_y, [plane_a[k * line_rows : (k + 1) * line_rows] for k in range(ring)]
    )
    line_b = small_scatter(
        to_x, [plane_b[k * line_rows : (k + 1) * line_rows] for k in range(ring)]
    )

    def split(v):
        top = lax.reduce_precision(v, 8, 7)
        return jnp.concatenate([top, v - top], axis=0).astype(jnp.bfloat16)

    def joined(v):
        v = v.astype(jnp.float32)
        return v[:local_experts] + v[local_experts : 2 * local_experts]

    tail = jnp.pad(split(peaks), ((0, rows - 2 * local_experts), (0, 0)))
    tail = jnp.broadcast_to(tail[None], (members, rows, lane))
    message = jnp.concatenate([line_a, line_b], axis=1).reshape(members, rows, half)
    message = jnp.concatenate([message, tail], axis=2)
    back = lax.all_to_all(message, "edata", split_axis=0, concat_axis=0, tiled=True)
    hidden_amax = jnp.max(jax.vmap(joined)(back[:, :, half:]), axis=(0, 2))
    total = jnp.sum(
        back[:, :, :half].reshape(members // 2, 2, rows, half).astype(jnp.float32), axis=0
    )
    layer_out = jnp.concatenate([total[0], total[1]], axis=1).astype(jnp.bfloat16)
    return (layer_out, hidden_amax)


def solution(mesh):
    return jax.shard_map(
        per_device,
        mesh=mesh,
        in_specs=(
            P(("expert", "edata"), None),
            P(("expert", "edata"), None),
            P(("expert", "edata"), None),
            P("expert", None, "edata"),
            P("expert", None, "edata"),
            P("expert", "edata", None),
            P("expert"),
        ),
        out_specs=(P(("expert", "edata"), None), P("expert")),
        check_vma=False,
    )
```

```python
import jax
import jax.numpy as jnp
from jax import lax
from jax.sharding import PartitionSpec as P


quant_limit = 448.0
lane = 128
ring = 4


def per_device(tokens, routes, combine, w_gate, w_up, w_down, past_amax):
    groups = lax.axis_size("expert")
    members = lax.axis_size("edata")
    local_experts, model_width, hidden_units = w_gate.shape
    rows = tokens.shape[0]
    half = model_width // 2
    fan = local_experts * hidden_units
    core = lax.axis_index("edata") % 2
    group = lax.axis_index("expert")
    swap = [(i, i ^ 1) for i in range(members)]

    def pair(v):
        return lax.ppermute(v, "edata", swap)

    def shift(v, k, outer):
        moves = []
        for e in range(groups):
            for i in range(members):
                if (i % 2 == 0) == outer:
                    to = (e // ring + k) % ring * ring + e % ring
                else:
                    to = e // ring * ring + (e % ring + k) % ring
                moves.append((e * members + i, to * members + i))
        return lax.ppermute(v, ("expert", "edata"), moves)

    def inner(v, k):
        return shift(v, k, False)

    def outer(v, k):
        return shift(v, k, True)

    def small_gather(send, block):
        behind = send(block, 1)
        return [block, send(block, -1), send(behind, 1), behind]

    def ring_gather(send, low, high, ready):
        behind_low, ahead_high = send(low, 1), send(high, -1)
        behind_high, ahead_low = send(high, 1), send(low, -1)
        behind_low, ahead_high, ready = lax.optimization_barrier(
            (behind_low, ahead_high, ready)
        )
        far = [send(behind_low, 1), send(ahead_high, -1)]
        halves = [low, high, ahead_low, ahead_high, *far, behind_low, behind_high]
        return halves, ready

    def add(*parts):
        return sum(p.astype(jnp.float32) for p in parts).astype(jnp.bfloat16)

    def small_scatter(send, blocks):
        behind = send(blocks[3], -1)
        return add(blocks[0], behind, send(add(blocks[1], send(blocks[2], 1)), 1))

    def ring_scatter(send, blocks):
        cut = blocks[0].shape[0] // 2
        low, high = [b[:cut] for b in blocks], [b[cut:] for b in blocks]
        far_low, far_high = send(low[2], 1), send(high[2], -1)
        got_high, got_low = send(high[1], 1), send(low[3], -1)
        sums = lax.optimization_barrier((add(low[1], far_low), add(high[3], far_high)))
        last_low, last_high = send(sums[0], 1), send(sums[1], -1)
        return add(low[0], got_low, last_low), add(high[0], got_high, last_high)

    lanes = jnp.arange(lane, dtype=jnp.int32)
    hits = routes[:, :, None] == lanes[None, None, :]
    weights = jnp.sum(jnp.where(hits, combine.astype(jnp.float32)[:, :, None], 0.0), axis=1)
    weights = weights.astype(jnp.bfloat16)

    pieces = jnp.stack(
        [
            jnp.concatenate([tokens[:, :half], weights], axis=1),
            jnp.concatenate([tokens[:, half:], weights], axis=1),
        ]
    )
    outgoing = jnp.broadcast_to(pieces[None], (members // 2, 2, rows, half + lane))
    outgoing = outgoing.reshape(members, rows, half + lane)
    line = lax.all_to_all(outgoing, "edata", split_axis=0, concat_axis=0, tiled=True)
    line = line.reshape(members * rows, half + lane)
    line_rows = members * rows

    plane = small_gather(inner, line)
    low, high = [jnp.concatenate(plane[k : k + 2], axis=0) for k in (0, 2)]
    low, high, w_gate, w_up, w_down = lax.optimization_barrier(
        (low, high, w_gate, w_up, w_down)
    )

    def joined_half(side):
        cut = [
            lax.dynamic_slice_in_dim(w, side * half, half, axis=1)[j]
            for w in (w_gate, w_up)
            for j in range(local_experts)
        ]
        return jnp.concatenate(cut, axis=1)

    def down_half(side):
        return lax.dynamic_slice_in_dim(w_down, side * half, half, axis=2).reshape(fan, half)

    w_own = joined_half(core)
    other_half = joined_half(1 - core)
    other_down = down_half(1 - core)
    w_other = pair(other_half)
    down_got = pair(other_down)
    down_own = down_half(core)

    blocks, (w_own, down_own, down_got) = ring_gather(outer, low, high, (w_own, down_own, down_got))
    w_out = jnp.concatenate([down_own, down_got], axis=0)
    everyone = jnp.concatenate(blocks, axis=0)

    def project(w):
        return jnp.dot(everyone[:, :half], w, preferred_element_type=jnp.float32)

    def swapped(v):
        v = v.reshape(ring, ring, line_rows, v.shape[1])
        return v.swapaxes(0, 1).reshape(ring * ring * line_rows, v.shape[3])

    unit_expert = jnp.arange(fan, dtype=jnp.int32) // hidden_units
    spread = (lanes[:, None] == group * local_experts + unit_expert[None, :]).astype(jnp.bfloat16)
    quant_gain = jnp.repeat(quant_limit / past_amax, hidden_units)
    dequant = jnp.repeat(past_amax / quant_limit, hidden_units)

    got = swapped(pair(project(w_other)))
    weight = jnp.dot(everyone[:, half:], spread, preferred_element_type=jnp.float32)
    both_proj = lax.optimization_barrier(project(w_own)) + got
    gate_proj = both_proj[:, :fan]
    up_proj = both_proj[:, fan:]
    hidden = jax.nn.silu(gate_proj) * up_proj
    peaks = jnp.max(jnp.where(weight > 0.0, jnp.abs(hidden), 0.0), axis=0)
    peaks = jnp.pad(peaks.reshape(local_experts, hidden_units), ((0, 0), (0, lane - hidden_units)))
    clipped = jnp.clip(hidden * quant_gain[None, :], -quant_limit, quant_limit)
    scaled = (clipped * (weight * dequant[None, :])).astype(jnp.bfloat16)
    both = jnp.concatenate([scaled, swapped(pair(scaled))], axis=1)
    down = jnp.dot(both, w_out, preferred_element_type=jnp.float32).astype(jnp.bfloat16)

    low, high = ring_scatter(outer, jnp.split(down, ring))
    line_sum = small_scatter(inner, [*jnp.split(low, 2), *jnp.split(high, 2)])

    def split(v):
        top = lax.reduce_precision(v, 8, 7)
        return jnp.concatenate([top, v - top], axis=0).astype(jnp.bfloat16)

    def joined(v):
        v = v.astype(jnp.float32)
        return v[:local_experts] + v[local_experts : 2 * local_experts]

    tail = jnp.pad(split(peaks), ((0, rows - 2 * local_experts), (0, 0)))
    tail = jnp.broadcast_to(tail[None], (members, rows, lane))
    message = line_sum.reshape(members, rows, half)
    message = jnp.concatenate([message, tail], axis=2)
    back = lax.all_to_all(message, "edata", split_axis=0, concat_axis=0, tiled=True)
    hidden_amax = jnp.max(jax.vmap(joined)(back[:, :, half:]), axis=(0, 2))
    total = jnp.sum(
        back[:, :, :half].reshape(members // 2, 2, rows, half).astype(jnp.float32), axis=0
    )
    layer_out = jnp.concatenate([total[0], total[1]], axis=1).astype(jnp.bfloat16)
    return (layer_out, hidden_amax)


def solution(mesh):
    return jax.shard_map(
        per_device,
        mesh=mesh,
        in_specs=(
            P(("expert", "edata"), None),
            P(("expert", "edata"), None),
            P(("expert", "edata"), None),
            P("expert", None, "edata"),
            P("expert", None, "edata"),
            P("expert", "edata", None),
            P("expert"),
        ),
        out_specs=(P(("expert", "edata"), None), P("expert")),
        check_vma=False,
    )
```

```python
import jax
import jax.numpy as jnp
from jax import lax
from jax.sharding import PartitionSpec as P


quant_limit = 448.0
lane = 128
ring = 4


def per_device(tokens, routes, combine, w_gate, w_up, w_down, past_amax):
    groups = lax.axis_size("expert")
    members = lax.axis_size("edata")
    local_experts, model_width, hidden_units = w_gate.shape
    rows = tokens.shape[0]
    half = model_width // 2
    fan = local_experts * hidden_units
    core = lax.axis_index("edata") % 2
    group = lax.axis_index("expert")
    swap = [(i, i ^ 1) for i in range(members)]

    def pair(v):
        return lax.ppermute(v, "edata", swap)

    def shift(v, k, outer):
        moves = []
        for e in range(groups):
            for i in range(members):
                if (i % 2 == 0) == outer:
                    to = (e // ring + k) % ring * ring + e % ring
                else:
                    to = e // ring * ring + (e % ring + k) % ring
                moves.append((e * members + i, to * members + i))
        return lax.ppermute(v, ("expert", "edata"), moves)

    def inner(v, k):
        return shift(v, k, False)

    def outer(v, k):
        return shift(v, k, True)

    def ring_gather(send, low, high, ready=()):
        behind_low, ahead_high = send(low, 1), send(high, -1)
        behind_high, ahead_low = send(high, 1), send(low, -1)
        behind_low, ahead_high, ready = lax.optimization_barrier(
            (behind_low, ahead_high, ready)
        )
        far = [send(behind_low, 1), send(ahead_high, -1)]
        halves = [low, high, ahead_low, ahead_high, behind_low, behind_high, *far]
        return halves, ready

    def add(*parts):
        return sum(p.astype(jnp.float32) for p in parts).astype(jnp.bfloat16)

    def ring_scatter(send, own, ahead, behind, far):
        cut = own.shape[0] // 2
        far_low, far_high = send(far[:cut], 1), send(far[cut:], -1)
        got_high, got_low = send(ahead[cut:], 1), send(behind[:cut], -1)
        sums = lax.optimization_barrier((add(ahead[:cut], far_low), add(behind[cut:], far_high)))
        last_low, last_high = send(sums[0], 1), send(sums[1], -1)
        return add(own[:cut], got_low, last_low), add(own[cut:], got_high, last_high)

    lanes = jnp.arange(lane, dtype=jnp.int32)
    hits = routes[:, :, None] == lanes[None, None, :]
    weights = jnp.sum(jnp.where(hits, combine.astype(jnp.float32)[:, :, None], 0.0), axis=1)
    weights = weights.astype(jnp.bfloat16)

    pieces = jnp.stack(
        [
            jnp.concatenate([tokens[:, :half], weights], axis=1),
            jnp.concatenate([tokens[:, half:], weights], axis=1),
        ]
    )
    outgoing = jnp.broadcast_to(pieces[None], (members // 2, 2, rows, half + lane))
    outgoing = outgoing.reshape(members, rows, half + lane)
    line = lax.all_to_all(outgoing, "edata", split_axis=0, concat_axis=0, tiled=True)
    line = line.reshape(members * rows, half + lane)
    line_rows = members * rows

    plane, _ = ring_gather(inner, *jnp.split(line, 2))
    low, high = jnp.concatenate(plane[:4], axis=0), jnp.concatenate(plane[4:], axis=0)
    low, high, w_gate, w_up, w_down = lax.optimization_barrier(
        (low, high, w_gate, w_up, w_down)
    )

    def joined_half(side):
        cut = [
            lax.dynamic_slice_in_dim(w, side * half, half, axis=1)[j]
            for w in (w_gate, w_up)
            for j in range(local_experts)
        ]
        return jnp.concatenate(cut, axis=1)

    def down_half(side):
        return lax.dynamic_slice_in_dim(w_down, side * half, half, axis=2).reshape(fan, half)

    w_own = joined_half(core)
    other_half = joined_half(1 - core)
    other_down = down_half(1 - core)
    w_other = pair(other_half)
    down_got = pair(other_down)
    down_own = down_half(core)

    blocks, (w_own, down_own, down_got) = ring_gather(outer, low, high, (w_own, down_own, down_got))
    w_out = jnp.concatenate([down_own, down_got], axis=0)
    row_parts = [jnp.concatenate(b, axis=0) for b in (blocks[:6], blocks[6:])]

    def project(w):
        def dot(part):
            return jnp.dot(part[:, :half], w, preferred_element_type=jnp.float32)

        near = dot(row_parts[0])
        return near, dot(row_parts[1])

    def swapped(v):
        v = v.reshape(ring, ring, line_rows, v.shape[1])
        return v.swapaxes(0, 1).reshape(ring * ring * line_rows, v.shape[3])

    unit_expert = jnp.arange(fan, dtype=jnp.int32) // hidden_units
    spread = (lanes[:, None] == group * local_experts + unit_expert[None, :]).astype(jnp.bfloat16)
    quant_gain = jnp.repeat(quant_limit / past_amax, hidden_units)
    dequant = jnp.repeat(past_amax / quant_limit, hidden_units)

    got = [pair(part) for part in project(w_other)]
    own = [lax.optimization_barrier(part) for part in project(w_own)]
    weight = jnp.dot(
        jnp.concatenate([part[:, half:] for part in row_parts], axis=0),
        spread,
        preferred_element_type=jnp.float32,
    )
    both_proj = jnp.concatenate(own, axis=0) + swapped(jnp.concatenate(got, axis=0))
    gate_proj = both_proj[:, :fan]
    up_proj = both_proj[:, fan:]
    hidden = jax.nn.silu(gate_proj) * up_proj
    peaks = jnp.max(jnp.where(weight > 0.0, jnp.abs(hidden), 0.0), axis=0)
    peaks = jnp.pad(peaks.reshape(local_experts, hidden_units), ((0, 0), (0, lane - hidden_units)))
    clipped = jnp.clip(hidden * quant_gain[None, :], -quant_limit, quant_limit)
    scaled = (clipped * (weight * dequant[None, :])).astype(jnp.bfloat16)
    both = jnp.concatenate([scaled, swapped(pair(scaled))], axis=1)
    down = jnp.dot(both, w_out, preferred_element_type=jnp.float32).astype(jnp.bfloat16)

    low, high = ring_scatter(outer, *jnp.split(down, ring))
    line_sum = ring_scatter(inner, *jnp.split(low, 2), *jnp.split(high, 2))
    line_sum = jnp.concatenate(line_sum, axis=0)

    def split(v):
        top = lax.reduce_precision(v, 8, 7)
        return jnp.concatenate([top, v - top], axis=0).astype(jnp.bfloat16)

    def joined(v):
        v = v.astype(jnp.float32)
        return v[:local_experts] + v[local_experts : 2 * local_experts]

    tail = jnp.pad(split(peaks), ((0, rows - 2 * local_experts), (0, 0)))
    tail = jnp.broadcast_to(tail[None], (members, rows, lane))
    message = line_sum.reshape(members, rows, half)
    message = jnp.concatenate([message, tail], axis=2)
    back = lax.all_to_all(message, "edata", split_axis=0, concat_axis=0, tiled=True)
    hidden_amax = jnp.max(jax.vmap(joined)(back[:, :, half:]), axis=(0, 2))
    total = jnp.sum(
        back[:, :, :half].reshape(members // 2, 2, rows, half).astype(jnp.float32), axis=0
    )
    layer_out = jnp.concatenate([total[0], total[1]], axis=1).astype(jnp.bfloat16)
    return (layer_out, hidden_amax)


def solution(mesh):
    return jax.shard_map(
        per_device,
        mesh=mesh,
        in_specs=(
            P(("expert", "edata"), None),
            P(("expert", "edata"), None),
            P(("expert", "edata"), None),
            P("expert", None, "edata"),
            P("expert", None, "edata"),
            P("expert", "edata", None),
            P("expert"),
        ),
        out_specs=(P(("expert", "edata"), None), P("expert")),
        check_vma=False,
    )
```

```python
import jax
import jax.numpy as jnp
from jax import lax
from jax.sharding import PartitionSpec as P


quant_limit = 448.0
lane = 128
ring = 4


def per_device(tokens, routes, combine, w_gate, w_up, w_down, past_amax):
    groups = lax.axis_size("expert")
    members = lax.axis_size("edata")
    local_experts, model_width, hidden_units = w_gate.shape
    rows = tokens.shape[0]
    half = model_width // 2
    fan = local_experts * hidden_units
    core = lax.axis_index("edata") % 2
    group = lax.axis_index("expert")
    swap = [(i, i ^ 1) for i in range(members)]

    def pair(v):
        return lax.ppermute(v, "edata", swap)

    def shift(v, k, outer):
        moves = []
        for e in range(groups):
            for i in range(members):
                if (i % 2 == 0) == outer:
                    to = (e // ring + k) % ring * ring + e % ring
                else:
                    to = e // ring * ring + (e % ring + k) % ring
                moves.append((e * members + i, to * members + i))
        return lax.ppermute(v, ("expert", "edata"), moves)

    def inner(v, k):
        return shift(v, k, False)

    def outer(v, k):
        return shift(v, k, True)

    def ring_gather(send, low, high, ready=()):
        behind_low, ahead_high = send(low, 1), send(high, -1)
        behind_high, ahead_low = send(high, 1), send(low, -1)
        behind_low, ahead_high, ready = lax.optimization_barrier(
            (behind_low, ahead_high, ready)
        )
        far = [send(behind_low, 1), send(ahead_high, -1)]
        near = [low, high, ahead_low, ahead_high, behind_low, behind_high]
        return [*lax.optimization_barrier(near), *far], ready

    def add(*parts):
        return sum(p.astype(jnp.float32) for p in parts).astype(jnp.bfloat16)

    def ring_scatter(send, own, ahead, behind, far):
        cut = own.shape[0] // 2
        far_low, far_high = send(far[:cut], 1), send(far[cut:], -1)
        got_high, got_low = send(ahead[cut:], 1), send(behind[:cut], -1)
        sums = lax.optimization_barrier((add(ahead[:cut], far_low), add(behind[cut:], far_high)))
        last_low, last_high = send(sums[0], 1), send(sums[1], -1)
        return add(own[:cut], got_low, last_low), add(own[cut:], got_high, last_high)

    lanes = jnp.arange(lane, dtype=jnp.int32)
    hits = routes[:, :, None] == lanes[None, None, :]
    weights = jnp.sum(jnp.where(hits, combine.astype(jnp.float32)[:, :, None], 0.0), axis=1)
    weights = weights.astype(jnp.bfloat16)

    pieces = jnp.stack(
        [
            jnp.concatenate([tokens[:, :half], weights], axis=1),
            jnp.concatenate([tokens[:, half:], weights], axis=1),
        ]
    )
    outgoing = jnp.broadcast_to(pieces[None], (members // 2, 2, rows, half + lane))
    outgoing = outgoing.reshape(members, rows, half + lane)
    line = lax.all_to_all(outgoing, "edata", split_axis=0, concat_axis=0, tiled=True)
    line = line.reshape(members * rows, half + lane)
    line_rows = members * rows

    plane, _ = ring_gather(inner, *jnp.split(line, 2))
    low, high = jnp.concatenate(plane[:4], axis=0), jnp.concatenate(plane[4:], axis=0)
    low, high, w_gate, w_up, w_down = lax.optimization_barrier(
        (low, high, w_gate, w_up, w_down)
    )

    def joined_half(side):
        cut = [
            lax.dynamic_slice_in_dim(w, side * half, half, axis=1)[j]
            for w in (w_gate, w_up)
            for j in range(local_experts)
        ]
        return jnp.concatenate(cut, axis=1)

    def down_half(side):
        return lax.dynamic_slice_in_dim(w_down, side * half, half, axis=2).reshape(fan, half)

    w_own = joined_half(core)
    other_half = joined_half(1 - core)
    other_down = down_half(1 - core)
    w_other = pair(other_half)
    down_got = pair(other_down)
    down_own = down_half(core)

    blocks, (w_own, down_own, down_got) = ring_gather(outer, low, high, (w_own, down_own, down_got))
    w_out = jnp.concatenate([down_own, down_got], axis=0)
    row_parts = [jnp.concatenate(b, axis=0) for b in (blocks[:6], blocks[6:])]

    def project(w):
        def dot(part):
            return jnp.dot(part[:, :half], w, preferred_element_type=jnp.float32)

        near = dot(row_parts[0])
        return near, dot(row_parts[1])

    def swapped(v):
        v = v.reshape(ring, ring, line_rows, v.shape[1])
        return v.swapaxes(0, 1).reshape(ring * ring * line_rows, v.shape[3])

    unit_expert = jnp.arange(fan, dtype=jnp.int32) // hidden_units
    spread = (lanes[:, None] == group * local_experts + unit_expert[None, :]).astype(jnp.bfloat16)
    quant_gain = jnp.repeat(quant_limit / past_amax, hidden_units)
    dequant = jnp.repeat(past_amax / quant_limit, hidden_units)

    got = [pair(part) for part in project(w_other)]
    own = [lax.optimization_barrier(part) for part in project(w_own)]
    weight = jnp.dot(
        jnp.concatenate([part[:, half:] for part in row_parts], axis=0),
        spread,
        preferred_element_type=jnp.float32,
    )
    both_proj = jnp.concatenate(own, axis=0) + swapped(jnp.concatenate(got, axis=0))
    gate_proj = both_proj[:, :fan]
    up_proj = both_proj[:, fan:]
    hidden = jax.nn.silu(gate_proj) * up_proj
    peaks = jnp.max(jnp.where(weight > 0.0, jnp.abs(hidden), 0.0), axis=0)
    peaks = jnp.pad(peaks.reshape(local_experts, hidden_units), ((0, 0), (0, lane - hidden_units)))
    clipped = jnp.clip(hidden * quant_gain[None, :], -quant_limit, quant_limit)
    scaled = (clipped * (weight * dequant[None, :])).astype(jnp.bfloat16)
    both = jnp.concatenate([scaled, swapped(pair(scaled))], axis=1)
    cut = both.shape[0] // ring * (ring - 1)

    def down(part):
        return jnp.dot(part, w_out, preferred_element_type=jnp.float32).astype(jnp.bfloat16)

    rest = down(both[:cut])
    down_blocks = [*jnp.split(rest, ring - 1), down(both[cut:])]

    low, high = ring_scatter(outer, *down_blocks)
    line_sum = ring_scatter(inner, *jnp.split(low, 2), *jnp.split(high, 2))
    line_sum = jnp.concatenate(line_sum, axis=0)

    def split(v):
        top = lax.reduce_precision(v, 8, 7)
        return jnp.concatenate([top, v - top], axis=0).astype(jnp.bfloat16)

    def joined(v):
        v = v.astype(jnp.float32)
        return v[:local_experts] + v[local_experts : 2 * local_experts]

    tail = jnp.pad(split(peaks), ((0, rows - 2 * local_experts), (0, 0)))
    tail = jnp.broadcast_to(tail[None], (members, rows, lane))
    message = line_sum.reshape(members, rows, half)
    message = jnp.concatenate([message, tail], axis=2)
    back = lax.all_to_all(message, "edata", split_axis=0, concat_axis=0, tiled=True)
    hidden_amax = jnp.max(jax.vmap(joined)(back[:, :, half:]), axis=(0, 2))
    total = jnp.sum(
        back[:, :, :half].reshape(members // 2, 2, rows, half).astype(jnp.float32), axis=0
    )
    layer_out = jnp.concatenate([total[0], total[1]], axis=1).astype(jnp.bfloat16)
    return (layer_out, hidden_amax)


def solution(mesh):
    return jax.shard_map(
        per_device,
        mesh=mesh,
        in_specs=(
            P(("expert", "edata"), None),
            P(("expert", "edata"), None),
            P(("expert", "edata"), None),
            P("expert", None, "edata"),
            P("expert", None, "edata"),
            P("expert", "edata", None),
            P("expert"),
        ),
        out_specs=(P(("expert", "edata"), None), P("expert")),
        check_vma=False,
    )
```
